32 devices in a mesh: groups: 2 (over y), seg: 4 (over z), ch: 2 (over x), sub: 2 (over core).
Axes of the slice: x: 2, y: 2, z: 4, core: 2. Of those that a mesh axis runs over, the one named last changes fastest.
Arguments:
- rank_series: bfloat16 [2048, 16384], P(('groups', 'ch', 'sub'), 'seg'), parts along dimension 0, may hold values from -6 to 6
- power_series: bfloat16 [2048, 16384], P(('groups', 'ch', 'sub'), 'seg'), parts along dimension 0, may hold values from -6 to 6
- seg_offsets: int32 [32], P(('groups', 'seg')), parts along dimension 0, may hold values from 2048 to 4095, as said below
- bin_index: int32 [128], replicated, may hold values from 0 to 511, as said below
Outputs:
- cross_spectra: bfloat16 [2, 256, 1024, 1024], P(None, ('groups', 'seg'), ('ch', 'sub')), parts along dimension 1
The draws below stay inside these ranges and needn't reach their ends.
There are 2 independent parts, one for each index of `groups`. The reference program is written for one: setup_inputs(seed, part) draws one part's arguments, and reference() takes and returns one part's arrays. A program takes and returns all parts, laid end to end along the dimension named above; an argument that names none is the same for every part. Nothing has to cross between parts.
Inputs may be any that keep to these rules, and one draw needn't show every extreme that they name: `seg_offsets`: every segment reads at least half of its samples past its own 4096 samples, in the following ones. `bin_index`: the bins are distinct.
All inputs are finite; a program needn't handle non-finite values.
Results may differ from the reference program's by a relative error of at most 0.0055.
Values may be sent and summed in bfloat16 or wider, within the bound.
A program may use at most 192 MiB of HBM per device.

```python
import math
import jax
import jax.numpy as jnp
from jax import lax

R = 1024
P_SIZE = 1024
LEN = 4096
BINS = 128
SEG_DEV = 4
SEGS = 16
SAMPLES = 16384


def draw_seg_offsets(key, part):
    values = jax.random.randint(key, (SEGS,), LEN // 2, LEN, dtype=jnp.int32)
    return values.at[0].set(LEN - 1).at[1].set(LEN // 2)


def draw_bin_index(key, part):
    shuffled = jax.random.permutation(key, 4 * BINS - 2).astype(jnp.int32) + 1
    ends = jnp.array([0, 4 * BINS - 1], dtype=jnp.int32)
    return jnp.concatenate([ends, shuffled[:BINS - 2]])


def steps_of(stream_key, extent, split, smallest, largest):
    gain = 1.0
    for dim, shards_of in split:
        steps = jax.random.uniform(jax.random.fold_in(jax.random.fold_in(stream_key, 6), dim), (shards_of,), jnp.float32, smallest / len(split), largest / len(split))
        gain = gain * jnp.repeat(jnp.exp(steps), extent[dim] // shards_of).reshape((-1,) + (1,) * (len(extent) - 1 - dim))
    return gain


def bell_draw(rng, shape, spread, bound, split=(), held_as=jnp.bfloat16):
    loudness = steps_of(rng, shape, split, -0.22, 0.18) if split else 1.0
    drawn = jax.random.normal(rng, shape, jnp.float32) * spread * loudness
    return jnp.minimum(jnp.maximum(drawn, -bound), bound).astype(held_as)


def setup_inputs(seed: int = 0, part: int = 0) -> dict:
    streams_of = jax.random.split(jax.random.key(seed), 5)
    part_splits = jax.random.split(jax.random.fold_in(streams_of[4], part), 5)
    rank_series = bell_draw(part_splits[0], (R, SAMPLES), 1.0, 6.0, ((0, 4), (1, 4)))
    power_series = bell_draw(part_splits[1], (P_SIZE, SAMPLES), 1.0, 6.0, ((0, 4), (1, 4)))
    seg_offsets = draw_seg_offsets(jax.random.fold_in(jax.random.fold_in(streams_of[4], part), 71), part)
    bin_index = draw_bin_index(jax.random.fold_in(streams_of[4], 71), part)
    return dict(rank_series=rank_series, power_series=power_series, seg_offsets=seg_offsets, bin_index=bin_index)


def make_kernel(bin_index):
    sample_ids = jnp.arange(LEN, dtype=jnp.int32)
    window = 0.5 - 0.5 * jnp.cos((2.0 * math.pi / LEN) * sample_ids.astype(jnp.float32))
    phase = (bin_index.astype(jnp.int32)[:, None] * sample_ids[None, :]) % LEN
    angle = (2.0 * math.pi / LEN) * phase.astype(jnp.float32)
    factor = (3.0 * LEN / 8.0) ** -0.5
    waves = jnp.stack([jnp.cos(angle), -jnp.sin(angle)]) * factor
    return (waves * window).astype(jnp.bfloat16)


def reference(rank_series, power_series, seg_offsets, bin_index):
    kernel = make_kernel(bin_index).astype(jnp.float32)
    starts = (jnp.arange(SEGS, dtype=jnp.int32) // SEG_DEV) * LEN + seg_offsets.astype(jnp.int32)

    def spectra(series):
        padded = jnp.concatenate([series, jnp.zeros((series.shape[0], LEN), series.dtype)], axis=1)

        def one_segment(start):
            segment = lax.dynamic_slice_in_dim(padded, start, LEN, 1).astype(jnp.float32)
            return jnp.einsum("tkn,cn->tkc", kernel, segment, precision=lax.Precision.HIGHEST)

        return lax.map(one_segment, starts).astype(jnp.bfloat16)

    rank_spectra = spectra(rank_series).astype(jnp.float32)
    power_spectra = spectra(power_series).astype(jnp.float32)
    swapped = jnp.stack([power_spectra[:, 1], -power_spectra[:, 0]], axis=1)
    real_part = jnp.einsum("gtkr,gtkp->krp", rank_spectra, power_spectra)
    imag_part = jnp.einsum("gtkr,gtkp->krp", rank_spectra, swapped)
    return jnp.stack([real_part, imag_part]).astype(jnp.bfloat16)
```

```python
import functools
import math

import jax
import jax.numpy as jnp
from jax import lax
from jax.experimental import pallas as pl
from jax.experimental.pallas import tpu as pltpu
from jax.sharding import PartitionSpec as P

LANES = 128
FINE = 64


def shifted(array, axis, by):
    peers = lax.axis_size(axis)
    pairs = [(i, i + by) for i in range(peers) if 0 <= i + by < peers]
    return lax.ppermute(array, axis, pairs)


def waves_of(bin_index, samples, length):
    freqs = jnp.stack([bin_index, jnp.ones_like(bin_index)])
    phase = freqs[:, None, :] * samples[None, :, None] % length
    angle = 2.0 * math.pi / length * phase.astype(jnp.float32)
    return jnp.stack([jnp.cos(angle), jnp.sin(angle)])


def spectra_kernel(
    length, head, chunk, off_ref, grid_ref, back_ref, rank_ref, power_ref, rank_out, power_out, acc, stage
):
    bins = grid_ref.shape[-1]
    width = rank_ref.shape[0]
    segs = off_ref.shape[0]
    first = 0 if head else length // 2
    coarse = length // FINE
    factor = (3.0 * length / 8.0) ** (-0.5)

    for g in range(segs):
        offset = off_ref[g]
        acc[...] = jnp.zeros_like(acc)
        moved = []
        for kind in range(2):
            cb = grid_ref[0, kind, coarse : coarse + FINE, :]
            sb = grid_ref[1, kind, coarse : coarse + FINE, :]
            co = back_ref[0, kind, g : g + 1, :]
            so = back_ref[1, kind, g : g + 1, :]
            moved.append((cb * co - sb * so, sb * co + cb * so))

        @pl.loop(0, (length - first) // chunk)
        def _(c):
            rows = []
            for piece in range(chunk // FINE):
                a = first // FINE + c * (chunk // FINE) + piece
                ca = grid_ref[0, 0, pl.ds(a, 1), :]
                sa = grid_ref[1, 0, pl.ds(a, 1), :]
                cw = grid_ref[0, 1, pl.ds(a, 1), :]
                sw = grid_ref[1, 1, pl.ds(a, 1), :]
                (cb, sb), (cv, sv) = moved
                window = (0.5 - 0.5 * (cw * cv - sw * sv)) * factor
                sample = lax.broadcasted_iota(jnp.int32, (FINE, bins), 0) + a * FINE
                inside = sample < offset if head else sample >= offset
                window = jnp.where(inside, window, 0.0)
                cosine = (ca * cb - sa * sb) * window
                sine = (sa * cb + ca * sb) * -window
                rows.append(jnp.concatenate([cosine, sine], axis=1).astype(jnp.bfloat16))
            col = pl.multiple_of(first + c * chunk, chunk)
            series = jnp.concatenate(
                [rank_ref[:, pl.ds(col, chunk)], power_ref[:, pl.ds(col, chunk)]], axis=0
            )
            acc[...] += jnp.dot(
                series, jnp.concatenate(rows, axis=0), preferred_element_type=jnp.float32
            )

        for t in range(2):
            for l in range(2 * width // LANES):
                part = acc[l * LANES : (l + 1) * LANES, t * bins : (t + 1) * bins]
                stage[l, pl.ds(t * segs + g, bins, stride=2 * segs), :] = part.T

    per = width // LANES
    for l in range(2 * per):
        out = rank_out if l < per else power_out
        lane = (l % per) * LANES
        out[:, :, lane : lane + LANES] = (
            stage[l].reshape(bins, 2 * segs, LANES).astype(out.dtype)
        )


def spectra(offsets, grid, bin_index, rank_series, power_series, head):
    width, length = rank_series.shape
    bins = grid.shape[-1]
    segs = offsets.shape[0]
    back = waves_of(bin_index, -offsets, length)
    dtype = jnp.bfloat16 if head else jnp.float32
    out = jax.ShapeDtypeStruct((bins, 2 * segs, width), dtype)
    rows = length if head else length // 2
    vmem = pl.BlockSpec(memory_space=pltpu.VMEM)
    return pl.pallas_call(
        functools.partial(spectra_kernel, length, head, 1024),
        out_shape=(out, out),
        in_specs=[pl.BlockSpec(memory_space=pltpu.SMEM), vmem, vmem, vmem, vmem],
        out_specs=(vmem, vmem),
        scratch_shapes=[
            pltpu.VMEM((2 * width, 2 * bins), jnp.float32),
            pltpu.VMEM((2 * width // LANES, bins * 2 * segs, LANES), jnp.float32),
        ],
        compiler_params=pltpu.CompilerParams(vmem_limit_bytes=40 << 20),
        cost_estimate=pl.CostEstimate(
            flops=2 * segs * rows * 2 * bins * 2 * width,
            bytes_accessed=2 * width * length * 2,
            transcendentals=0,
        ),
        name="head_spectra" if head else "own_spectra",
    )(offsets, grid, back, rank_series, power_series)


def cross_kernel(rank_ref, power_ref, out_ref):
    peers, block, rows, width = rank_ref.shape
    gathered = power_ref.shape[0]
    half = rows // 2
    depth = peers * rows
    for i in range(block):
        rank = rank_ref[:, i].astype(jnp.float32)
        turned = jnp.concatenate([-rank[:, half:], rank[:, :half]], axis=1)
        both = jnp.concatenate([rank.reshape(depth, width), turned.reshape(depth, width)], axis=1)
        both = both.astype(jnp.bfloat16)
        for d in range(gathered):
            power = power_ref[d, :, i].astype(jnp.float32).reshape(depth, width)
            sums = lax.dot_general(
                both,
                power.astype(jnp.bfloat16),
                (((0,), (0,)), ((), ())),
                preferred_element_type=jnp.float32,
            ).astype(out_ref.dtype)
            out_ref[0, i, :, d * width : (d + 1) * width] = sums[:width]
            out_ref[1, i, :, d * width : (d + 1) * width] = sums[width:]


def cross(rank_owned, power_all):
    peers, bins, rows, width = rank_owned.shape
    gathered = power_all.shape[0]
    block = 2
    return pl.pallas_call(
        cross_kernel,
        out_shape=jax.ShapeDtypeStruct((2, bins, width, gathered * width), jnp.bfloat16),
        grid=(bins // block,),
        in_specs=[
            pl.BlockSpec((peers, block, rows, width), lambda k: (0, k, 0, 0)),
            pl.BlockSpec((gathered, peers, block, rows, width), lambda k: (0, 0, k, 0, 0)),
        ],
        out_specs=pl.BlockSpec((2, block, width, gathered * width), lambda k: (0, k, 0, 0)),
        compiler_params=pltpu.CompilerParams(vmem_limit_bytes=48 << 20),
        name="cross_spectra",
    )(rank_owned, power_all)


def to_owners(array):
    peers = lax.axis_size("seg")
    split = array.reshape((peers, array.shape[0] // peers) + array.shape[1:])
    return lax.all_to_all(split, "seg", split_axis=0, concat_axis=0)


def body(rank_series, power_series, seg_offsets, bin_index):
    length = rank_series.shape[1]
    coarse = jnp.arange(0, length, FINE, dtype=jnp.int32)
    samples = jnp.concatenate([coarse, jnp.arange(FINE, dtype=jnp.int32)])
    grid = waves_of(bin_index, samples, length)
    before = shifted(seg_offsets, "seg", 1)
    rank_head, power_head = spectra(before, grid, bin_index, rank_series, power_series, True)
    power_head = shifted(power_head, "seg", -1)
    rank_head = shifted(rank_head, "seg", -1)
    rank_own, power_own = spectra(seg_offsets, grid, bin_index, rank_series, power_series, False)
    power_spectra = (power_own + power_head.astype(jnp.float32)).astype(jnp.bfloat16)
    rank_spectra = (rank_own + rank_head.astype(jnp.float32)).astype(jnp.bfloat16)
    power_all = lax.all_gather(to_owners(power_spectra), ("ch", "sub"), axis=0)
    return cross(to_owners(rank_spectra), power_all)


def solution(mesh):
    return jax.shard_map(
        body,
        mesh=mesh,
        in_specs=(
            P(("groups", "ch", "sub"), "seg"),
            P(("groups", "ch", "sub"), "seg"),
            P(("groups", "seg")),
            P(),
        ),
        out_specs=P(None, ("groups", "seg"), ("ch", "sub"), None),
        check_vma=False,
    )
```

```python
import functools
import math

import jax
import jax.numpy as jnp
from jax import lax
from jax.experimental import pallas as pl
from jax.experimental.pallas import tpu as pltpu
from jax.sharding import PartitionSpec as P

LANES = 128
FINE = 64


def shifted(array, axis, by):
    peers = lax.axis_size(axis)
    pairs = [(i, i + by) for i in range(peers) if 0 <= i + by < peers]
    return lax.ppermute(array, axis, pairs)


def waves_of(bin_index, samples, length):
    freqs = jnp.stack([bin_index, jnp.ones_like(bin_index)])
    phase = freqs[:, None, :] * samples[None, :, None] % length
    angle = 2.0 * math.pi / length * phase.astype(jnp.float32)
    return jnp.stack([jnp.cos(angle), jnp.sin(angle)])


def transform(length, head, chunk, off_ref, grid_ref, back_ref, rank_ref, power_ref, acc, stage):
    bins = grid_ref.shape[-1]
    width = rank_ref.shape[0]
    segs = off_ref.shape[0]
    first = 0 if head else length // 2
    coarse = length // FINE
    factor = (3.0 * length / 8.0) ** (-0.5)

    for g in range(segs):
        offset = off_ref[g]
        acc[...] = jnp.zeros_like(acc)
        moved = []
        for kind in range(2):
            cb = grid_ref[0, kind, coarse : coarse + FINE, :]
            sb = grid_ref[1, kind, coarse : coarse + FINE, :]
            co = back_ref[0, kind, g : g + 1, :]
            so = back_ref[1, kind, g : g + 1, :]
            moved.append((cb * co - sb * so, sb * co + cb * so))

        @pl.loop(0, (length - first) // chunk)
        def _(c):
            rows = []
            for piece in range(chunk // FINE):
                a = first // FINE + c * (chunk // FINE) + piece
                ca = grid_ref[0, 0, pl.ds(a, 1), :]
                sa = grid_ref[1, 0, pl.ds(a, 1), :]
                cw = grid_ref[0, 1, pl.ds(a, 1), :]
                sw = grid_ref[1, 1, pl.ds(a, 1), :]
                (cb, sb), (cv, sv) = moved
                window = (0.5 - 0.5 * (cw * cv - sw * sv)) * factor
                sample = lax.broadcasted_iota(jnp.int32, (FINE, bins), 0) + a * FINE
                inside = sample < offset if head else sample >= offset
                window = jnp.where(inside, window, 0.0)
                cosine = (ca * cb - sa * sb) * window
                sine = (sa * cb + ca * sb) * -window
                rows.append(jnp.concatenate([cosine, sine], axis=1).astype(jnp.bfloat16))
            col = pl.multiple_of(first + c * chunk, chunk)
            series = jnp.concatenate(
                [rank_ref[:, pl.ds(col, chunk)], power_ref[:, pl.ds(col, chunk)]], axis=0
            )
            acc[...] += jnp.dot(
                series, jnp.concatenate(rows, axis=0), preferred_element_type=jnp.float32
            )

        for t in range(2):
            for l in range(2 * width // LANES):
                part = acc[l * LANES : (l + 1) * LANES, t * bins : (t + 1) * bins]
                stage[l, pl.ds(t * segs + g, bins, stride=2 * segs), :] = part.T


def head_kernel(
    length, chunk, off_ref, grid_ref, back_ref, rank_ref, power_ref, power_out, rank_out, acc, stage
):
    transform(length, True, chunk, off_ref, grid_ref, back_ref, rank_ref, power_ref, acc, stage)
    peers, block, rows, width = rank_out.shape
    per = width // LANES
    for l in range(2 * per):
        out = rank_out if l < per else power_out
        lane = (l % per) * LANES
        out[:, :, :, lane : lane + LANES] = (
            stage[l].reshape(peers, block, rows, LANES).astype(out.dtype)
        )


def exchange_kernel(
    length, chunk, peers, plane, off_ref, grid_ref, back_ref, rank_ref, power_ref, power_head, rank_head,
    power_all, rank_owned, acc, stage, arrived, summed,
    head_send, head_recv, own_send, own_recv, plane_send, plane_recv,
):
    mesh_id = pl.DeviceIdType.MESH
    here = lax.axis_index("seg")
    fanout = plane[0] * plane[1]
    place = lax.axis_index("ch") * plane[1] + lax.axis_index("sub")
    block, rows, width = summed.shape[2:]
    per = width // LANES

    def along(z):
        return {"seg": z}

    def beside(q):
        return {"ch": q // plane[1], "sub": lax.rem(q, plane[1])}

    barrier = pltpu.get_barrier_semaphore()
    for i in range(1, peers):
        pl.semaphore_signal(
            barrier, inc=1, device_id=along(lax.rem(here + i, peers)), device_id_type=mesh_id
        )
    for i in range(1, fanout):
        pl.semaphore_signal(
            barrier, inc=1, device_id=beside(lax.rem(place + i, fanout)), device_id_type=mesh_id
        )
    pl.semaphore_wait(barrier, peers + fanout - 2)

    def head_copy(kind, owner):
        return pltpu.make_async_remote_copy(
            src_ref=(power_head, rank_head)[kind].at[owner],
            dst_ref=arrived.at[kind, owner],
            send_sem=head_send.at[kind, owner],
            recv_sem=head_recv.at[kind, owner],
            device_id=along(lax.rem(here + peers - 1, peers)),
            device_id_type=mesh_id,
        )

    def slot(kind, source):
        return power_all.at[place, source] if kind == 0 else rank_owned.at[source]

    def own_copy(kind, owner, source):
        return pltpu.make_async_remote_copy(
            src_ref=summed.at[kind, owner],
            dst_ref=slot(kind, source),
            send_sem=own_send.at[kind, owner],
            recv_sem=own_recv.at[kind, source],
            device_id=along(owner),
            device_id_type=mesh_id,
        )

    def plane_copy(source, sender, target):
        return pltpu.make_async_remote_copy(
            src_ref=power_all.at[sender, source],
            dst_ref=power_all.at[sender, source],
            send_sem=plane_send.at[source, target],
            recv_sem=plane_recv.at[source, sender],
            device_id=beside(target),
            device_id_type=mesh_id,
        )

    @pl.when(here > 0)
    def _():
        for kind in range(2):
            for i in range(peers):
                head_copy(kind, lax.rem(here + i, peers)).start()

    transform(length, False, chunk, off_ref, grid_ref, back_ref, rank_ref, power_ref, acc, stage)

    def total(kind, owner, out):
        def own(l):
            piece = stage[l + (0 if kind else per), pl.ds(owner * block * rows, block * rows), :]
            return piece.reshape(block, rows, LANES)

        @pl.when(here < peers - 1)
        def _():
            head_copy(kind, owner).wait_recv()
            for l in range(per):
                lanes = slice(l * LANES, (l + 1) * LANES)
                late = arrived[kind, owner, :, :, lanes].astype(jnp.float32)
                out[:, :, lanes] = (own(l) + late).astype(out.dtype)

        @pl.when(here == peers - 1)
        def _():
            for l in range(per):
                lanes = slice(l * LANES, (l + 1) * LANES)
                out[:, :, lanes] = own(l).astype(out.dtype)

    def forward(source):
        for i in range(1, fanout):
            plane_copy(source, place, lax.rem(place + i, fanout)).start()

    for i in range(peers - 1):
        owner = lax.rem(here + 1 + i, peers)
        total(0, owner, summed.at[0, owner])
        own_copy(0, owner, here).start()
    total(0, here, slot(0, here))
    forward(here)
    for i in range(peers - 1):
        owner = lax.rem(here + 1 + i, peers)
        total(1, owner, summed.at[1, owner])
        own_copy(1, owner, here).start()
        source = lax.rem(here + peers - 1 - i, peers)
        own_copy(0, owner, source).wait_recv()
        forward(source)
    total(1, here, slot(1, here))

    for i in range(peers - 1):
        owner = lax.rem(here + 1 + i, peers)
        own_copy(1, owner, lax.rem(here + peers - 1 - i, peers)).wait_recv()
        own_copy(0, owner, here).wait_send()
        own_copy(1, owner, here).wait_send()
    for z in range(peers):
        for i in range(1, fanout):
            other = lax.rem(place + i, fanout)
            plane_copy(z, other, place).wait_recv()
            plane_copy(z, place, other).wait_send()

    @pl.when(here > 0)
    def _():
        for kind in range(2):
            for i in range(peers):
                head_copy(kind, lax.rem(here + i, peers)).wait_send()


def transform_scratch(width, bins, segs):
    return [
        pltpu.VMEM((2 * width, 2 * bins), jnp.float32),
        pltpu.VMEM((2 * width // LANES, bins * 2 * segs, LANES), jnp.float32),
    ]


def transform_cost(series, bins, segs, rows):
    width, length = series.shape
    return pl.CostEstimate(
        flops=2 * segs * rows * 2 * bins * 2 * width,
        bytes_accessed=2 * width * length * 2,
        transcendentals=0,
    )


def head_spectra(offsets, grid, back, rank_series, power_series):
    width, length = rank_series.shape
    bins = grid.shape[-1]
    segs = offsets.shape[0]
    peers = lax.axis_size("seg")
    out = jax.ShapeDtypeStruct((peers, bins // peers, 2 * segs, width), jnp.bfloat16)
    vmem = pl.BlockSpec(memory_space=pltpu.VMEM)
    return pl.pallas_call(
        functools.partial(head_kernel, length, 1024),
        out_shape=(out, out),
        in_specs=[pl.BlockSpec(memory_space=pltpu.SMEM)] + [vmem] * 4,
        out_specs=(vmem, vmem),
        scratch_shapes=transform_scratch(width, bins, segs),
        compiler_params=pltpu.CompilerParams(vmem_limit_bytes=40 << 20),
        cost_estimate=transform_cost(rank_series, bins, segs, length),
        name="head_spectra",
    )(offsets, grid, back, rank_series, power_series)


def exchange(offsets, grid, back, rank_series, power_series, power_head, rank_head):
    width, length = rank_series.shape
    bins = grid.shape[-1]
    segs = offsets.shape[0]
    peers = lax.axis_size("seg")
    plane = (lax.axis_size("ch"), lax.axis_size("sub"))
    fanout = plane[0] * plane[1]
    shape = (bins // peers, 2 * segs, width)
    vmem = pl.BlockSpec(memory_space=pltpu.VMEM)
    dma = pltpu.SemaphoreType.DMA
    return pl.pallas_call(
        functools.partial(exchange_kernel, length, 1024, peers, plane),
        out_shape=(
            jax.ShapeDtypeStruct((fanout, peers) + shape, jnp.bfloat16),
            jax.ShapeDtypeStruct((peers,) + shape, jnp.bfloat16),
        ),
        in_specs=[pl.BlockSpec(memory_space=pltpu.SMEM)] + [vmem] * 6,
        out_specs=(vmem, vmem),
        scratch_shapes=transform_scratch(width, bins, segs)
        + [
            pltpu.VMEM((2, peers) + shape, jnp.bfloat16),
            pltpu.VMEM((2, peers) + shape, jnp.bfloat16),
            dma((2, peers)),
            dma((2, peers)),
            dma((2, peers)),
            dma((2, peers)),
            dma((peers, fanout)),
            dma((peers, fanout)),
        ],
        compiler_params=pltpu.CompilerParams(
            vmem_limit_bytes=48 << 20, collective_id=0, has_side_effects=True
        ),
        cost_estimate=transform_cost(rank_series, bins, segs, length // 2),
        name="exchange_spectra",
    )(offsets, grid, back, rank_series, power_series, power_head, rank_head)


def cross_kernel(rank_ref, power_ref, out_ref):
    peers, block, rows, width = rank_ref.shape
    gathered = power_ref.shape[0]
    half = rows // 2
    depth = peers * rows
    for i in range(block):
        rank = rank_ref[:, i].astype(jnp.float32)
        turned = jnp.concatenate([-rank[:, half:], rank[:, :half]], axis=1)
        both = jnp.concatenate([rank.reshape(depth, width), turned.reshape(depth, width)], axis=1)
        both = both.astype(jnp.bfloat16)
        for d in range(gathered):
            power = power_ref[d, :, i].astype(jnp.float32).reshape(depth, width)
            sums = lax.dot_general(
                both,
                power.astype(jnp.bfloat16),
                (((0,), (0,)), ((), ())),
                preferred_element_type=jnp.float32,
            ).astype(out_ref.dtype)
            out_ref[0, i, :, d * width : (d + 1) * width] = sums[:width]
            out_ref[1, i, :, d * width : (d + 1) * width] = sums[width:]


def cross(rank_owned, power_all):
    peers, bins, rows, width = rank_owned.shape
    gathered = power_all.shape[0]
    block = 2
    return pl.pallas_call(
        cross_kernel,
        out_shape=jax.ShapeDtypeStruct((2, bins, width, gathered * width), jnp.bfloat16),
        grid=(bins // block,),
        in_specs=[
            pl.BlockSpec((peers, block, rows, width), lambda k: (0, k, 0, 0)),
            pl.BlockSpec((gathered, peers, block, rows, width), lambda k: (0, 0, k, 0, 0)),
        ],
        out_specs=pl.BlockSpec((2, block, width, gathered * width), lambda k: (0, k, 0, 0)),
        compiler_params=pltpu.CompilerParams(vmem_limit_bytes=48 << 20),
        name="cross_spectra",
    )(rank_owned, power_all)


def body(rank_series, power_series, seg_offsets, bin_index):
    length = rank_series.shape[1]
    coarse = jnp.arange(0, length, FINE, dtype=jnp.int32)
    samples = jnp.concatenate([coarse, jnp.arange(FINE, dtype=jnp.int32)])
    grid = waves_of(bin_index, samples, length)
    before = shifted(seg_offsets, "seg", 1)
    back = waves_of(bin_index, -before, length)
    power_head, rank_head = head_spectra(before, grid, back, rank_series, power_series)
    back = waves_of(bin_index, -seg_offsets, length)
    power_all, rank_owned = exchange(
        seg_offsets, grid, back, rank_series, power_series, power_head, rank_head
    )
    return cross(rank_owned, power_all)


def solution(mesh):
    return jax.shard_map(
        body,
        mesh=mesh,
        in_specs=(
            P(("groups", "ch", "sub"), "seg"),
            P(("groups", "ch", "sub"), "seg"),
            P(("groups", "seg")),
            P(),
        ),
        out_specs=P(None, ("groups", "seg"), ("ch", "sub"), None),
        check_vma=False,
    )
```

```python
import functools
import math

import jax
import jax.numpy as jnp
from jax import lax
from jax.experimental import pallas as pl
from jax.experimental.pallas import tpu as pltpu
from jax.sharding import PartitionSpec as P

LANES = 128
FINE = 64


def waves_of(bin_index, samples, length):
    freqs = jnp.stack([bin_index, jnp.ones_like(bin_index)])
    phase = freqs[:, None, :] * samples[None, :, None] % length
    angle = 2.0 * math.pi / length * phase.astype(jnp.float32)
    return jnp.stack([jnp.cos(angle), jnp.sin(angle)])


def transform(length, head, chunk, grid_ref, back_ref, rank_ref, power_ref, acc, stage):
    bins = grid_ref.shape[-1]
    width = rank_ref.shape[0]
    segs = back_ref.shape[1]
    first = 0 if head else length // 2
    coarse = length // FINE
    factor = (3.0 * length / 8.0) ** (-0.5)

    for g in range(segs):
        acc[...] = jnp.zeros_like(acc)
        moved = []
        for kind in range(2):
            cb = grid_ref[0, kind, coarse : coarse + FINE, :]
            sb = grid_ref[1, kind, coarse : coarse + FINE, :]
            co = back_ref[kind, g : g + 1, :]
            so = back_ref[2 + kind, g : g + 1, :]
            moved.append((cb * co - sb * so, sb * co + cb * so))
        (cb, sb), (cv, sv) = moved
        cv, sv = cv * (0.5 * factor), sv * (0.5 * factor)
        nb, mb = -sb, -cb
        offset = back_ref[4, g : g + 1, :]
        within = lax.broadcasted_iota(jnp.int32, (FINE, bins), 0).astype(jnp.float32) - offset

        @pl.loop(0, (length - first) // chunk)
        def _(c):
            rows = []
            for piece in range(chunk // FINE):
                a = first // FINE + c * (chunk // FINE) + piece
                ca = grid_ref[0, 0, pl.ds(a, 1), :]
                sa = grid_ref[1, 0, pl.ds(a, 1), :]
                cw = grid_ref[0, 1, pl.ds(a, 1), :]
                sw = grid_ref[1, 1, pl.ds(a, 1), :]
                window = 0.5 * factor - (cw * cv - sw * sv)
                edge = -(a * FINE).astype(jnp.float32)
                inside = within < edge if head else within >= edge
                window = jnp.where(inside, window, 0.0)
                cosine = (ca * cb - sa * sb) * window
                sine = (sa * mb + ca * nb) * window
                rows.append(jnp.concatenate([cosine, sine], axis=1).astype(jnp.bfloat16))
            col = pl.multiple_of(first + c * chunk, chunk)
            series = jnp.concatenate(
                [rank_ref[:, pl.ds(col, chunk)], power_ref[:, pl.ds(col, chunk)]], axis=0
            )
            acc[...] += jnp.dot(
                series, jnp.concatenate(rows, axis=0), preferred_element_type=jnp.float32
            )

        for t in range(2):
            for l in range(2 * width // LANES):
                part = acc[l * LANES : (l + 1) * LANES, t * bins : (t + 1) * bins]
                stage[l, pl.ds(t * segs + g, bins, stride=2 * segs), :] = part.T


def exchange_kernel(
    length, chunk, peers, plane, grid_ref, back_ref, rank_hbm, power_hbm,
    power_all, rank_owned, acc, head_stage, own_stage, back_in, rank_ref, power_ref,
    near, from_above, from_below, summed,
    load_sem, back_sem, near_send, above_recv, below_recv, far_send, far_recv, plane_send, plane_recv,
):
    mesh_id = pl.DeviceIdType.MESH
    here = lax.axis_index("seg")
    above = lax.rem(here + 1, peers)
    below = lax.rem(here + peers - 1, peers)
    fanout = plane[0] * plane[1]
    place = lax.axis_index("ch") * plane[1] + lax.axis_index("sub")
    block, rows, width = summed.shape[2:]
    per = width // LANES
    inward = sorted(range(peers), key=lambda d: min(d, peers - 1 - d))

    loads = [
        pltpu.make_async_copy(rank_hbm, rank_ref, load_sem.at[0]),
        pltpu.make_async_copy(power_hbm, power_ref, load_sem.at[1]),
    ]
    for load in loads:
        load.start()

    def beside(q):
        return {"ch": q // plane[1], "sub": lax.rem(q, plane[1])}

    barrier = pltpu.get_barrier_semaphore()
    for i in range(1, peers):
        pl.semaphore_signal(
            barrier, inc=1, device_id={"seg": lax.rem(here + i, peers)}, device_id_type=mesh_id
        )
    for i in range(1, fanout):
        pl.semaphore_signal(
            barrier, inc=1, device_id=beside(lax.rem(place + i, fanout)), device_id_type=mesh_id
        )
    pl.semaphore_wait(barrier, peers + fanout - 2)

    back_copy = pltpu.make_async_remote_copy(
        src_ref=back_ref,
        dst_ref=back_in,
        send_sem=back_sem.at[0],
        recv_sem=back_sem.at[1],
        device_id={"seg": above},
        device_id_type=mesh_id,
    )

    def near_copy(kind, owner, up):
        return pltpu.make_async_remote_copy(
            src_ref=near.at[kind, owner],
            dst_ref=(from_below if up else from_above).at[kind, owner],
            send_sem=near_send.at[kind, owner],
            recv_sem=(below_recv if up else above_recv).at[kind, owner],
            device_id={"seg": above if up else below},
            device_id_type=mesh_id,
        )

    def slot(kind, group):
        return power_all.at[place, group] if kind == 0 else rank_owned.at[group]

    def far_copy(kind, owner, group):
        return pltpu.make_async_remote_copy(
            src_ref=summed.at[kind, owner],
            dst_ref=slot(kind, group),
            send_sem=far_send.at[kind, owner],
            recv_sem=far_recv.at[kind, group],
            device_id={"seg": owner},
            device_id_type=mesh_id,
        )

    def plane_copy(group, sender, target):
        return pltpu.make_async_remote_copy(
            src_ref=power_all.at[sender, group],
            dst_ref=power_all.at[sender, group],
            send_sem=plane_send.at[group, target],
            recv_sem=plane_recv.at[group, sender],
            device_id=beside(target),
            device_id_type=mesh_id,
        )

    def put(kind, owner, stage, late, out):
        for l in range(per):
            lanes = slice(l * LANES, (l + 1) * LANES)
            first = owner * block * rows
            piece = stage[l + (0 if kind else per), first : first + block * rows, :]
            piece = piece.reshape(block, rows, LANES)
            if late is not None:
                piece = piece + late[kind, owner, :, :, lanes].astype(jnp.float32)
            out[:, :, lanes] = piece.astype(out.dtype)

    def own_total(kind, owner, out):
        @pl.when(here < peers - 1)
        def _():
            near_copy(kind, owner, False).wait_recv()
            put(kind, owner, own_stage, from_above, out)

        @pl.when(here == peers - 1)
        def _():
            put(kind, owner, own_stage, None, out)

    def head_total(kind, owner, out):
        near_copy(kind, owner, True).wait_recv()
        put(kind, owner, head_stage, from_below, out)

    def forward(group):
        for i in range(1, fanout):
            plane_copy(group, place, lax.rem(place + i, fanout)).start()

    @pl.when(here < peers - 1)
    def _():
        back_copy.start()

    for load in loads:
        load.wait()

    @pl.when(here > 0)
    def _():
        back_copy.wait_recv()
        transform(length, True, chunk, grid_ref, back_in, rank_ref, power_ref, acc, head_stage)
        for kind in range(2):
            for d in range(peers - 1):
                @pl.when(d < here)
                def _():
                    put(kind, d, head_stage, None, near.at[kind, d])
                    near_copy(kind, d, False).start()

    transform(length, False, chunk, grid_ref, back_ref, rank_ref, power_ref, acc, own_stage)
    for kind in range(2):
        for d in reversed(range(1, peers)):
            @pl.when(d > here)
            def _():
                put(kind, d, own_stage, None, near.at[kind, d])
                near_copy(kind, d, True).start()

    for kind in range(2):
        for d in inward:
            @pl.when(d < here)
            def _():
                own_total(kind, d, summed.at[kind, d])
                far_copy(kind, d, here).start()

            @pl.when((d > here) & (here > 0))
            def _():
                head_total(kind, d, summed.at[kind, d])
                far_copy(kind, d, below).start()

        for d in range(peers):
            @pl.when(d == here)
            def _():
                own_total(kind, d, slot(kind, d))
                if kind == 0:
                    forward(d)
                if d > 0:
                    head_total(kind, d, slot(kind, d - 1))
                    if kind == 0:
                        forward(d - 1)

    def apart(group):
        return (group != here) & (group != here - 1)

    for group in reversed(inward):
        @pl.when(apart(group))
        def _():
            far_copy(0, here, group).wait_recv()
            forward(group)

    for group in range(peers):
        @pl.when(apart(group))
        def _():
            far_copy(1, here, group).wait_recv()

        for i in range(1, fanout):
            other = lax.rem(place + i, fanout)
            plane_copy(group, other, place).wait_recv()
            plane_copy(group, place, other).wait_send()

    for kind in range(2):
        for d in range(peers):
            @pl.when(d != here)
            def _():
                near_copy(kind, d, True).wait_send()

            @pl.when((d < here) | ((d > here) & (here > 0)))
            def _():
                far_copy(kind, d, 0).wait_send()

    @pl.when(here < peers - 1)
    def _():
        back_copy.wait_send()


def exchange(grid, back, rank_series, power_series):
    width, length = rank_series.shape
    bins = grid.shape[-1]
    segs = back.shape[1]
    peers = lax.axis_size("seg")
    plane = (lax.axis_size("ch"), lax.axis_size("sub"))
    fanout = plane[0] * plane[1]
    shape = (bins // peers, 2 * segs, width)
    vmem = pl.BlockSpec(memory_space=pltpu.VMEM)
    hbm = pl.BlockSpec(memory_space=pl.ANY)
    dma = pltpu.SemaphoreType.DMA
    stage = pltpu.VMEM((2 * width // LANES, bins * 2 * segs, LANES), jnp.float32)
    return pl.pallas_call(
        functools.partial(exchange_kernel, length, 1024, peers, plane),
        out_shape=(
            jax.ShapeDtypeStruct((fanout, peers) + shape, jnp.bfloat16),
            jax.ShapeDtypeStruct((peers,) + shape, jnp.bfloat16),
        ),
        in_specs=[vmem, vmem, hbm, hbm],
        out_specs=(vmem, vmem),
        scratch_shapes=[
            pltpu.VMEM((2 * width, 2 * bins), jnp.float32),
            stage,
            stage,
            pltpu.VMEM(back.shape, jnp.float32),
            pltpu.VMEM(rank_series.shape, jnp.bfloat16),
            pltpu.VMEM(power_series.shape, jnp.bfloat16),
        ]
        + [pltpu.VMEM((2, peers) + shape, jnp.bfloat16)] * 4
        + [dma((2,)), dma((2,))]
        + [dma((2, peers))] * 5
        + [dma((peers, fanout))] * 2,
        compiler_params=pltpu.CompilerParams(
            vmem_limit_bytes=56 << 20, collective_id=0, has_side_effects=True
        ),
        name="exchange_spectra",
    )(grid, back, rank_series, power_series)


def cross_kernel(rank_ref, power_ref, out_ref):
    peers, block, rows, width = rank_ref.shape
    gathered = power_ref.shape[0]
    half = rows // 2
    depth = peers * rows
    for i in range(block):
        rank = rank_ref[:, i].astype(jnp.float32)
        turned = jnp.concatenate([-rank[:, half:], rank[:, :half]], axis=1)
        both = jnp.concatenate([rank.reshape(depth, width), turned.reshape(depth, width)], axis=1)
        both = both.astype(jnp.bfloat16)
        for d in range(gathered):
            power = power_ref[d, :, i].astype(jnp.float32).reshape(depth, width)
            sums = lax.dot_general(
                both,
                power.astype(jnp.bfloat16),
                (((0,), (0,)), ((), ())),
                preferred_element_type=jnp.float32,
            ).astype(out_ref.dtype)
            out_ref[0, i, :, d * width : (d + 1) * width] = sums[:width]
            out_ref[1, i, :, d * width : (d + 1) * width] = sums[width:]


def cross(rank_owned, power_all):
    peers, bins, rows, width = rank_owned.shape
    gathered = power_all.shape[0]
    block = 2
    return pl.pallas_call(
        cross_kernel,
        out_shape=jax.ShapeDtypeStruct((2, bins, width, gathered * width), jnp.bfloat16),
        grid=(bins // block,),
        in_specs=[
            pl.BlockSpec((peers, block, rows, width), lambda k: (0, k, 0, 0)),
            pl.BlockSpec((gathered, peers, block, rows, width), lambda k: (0, 0, k, 0, 0)),
        ],
        out_specs=pl.BlockSpec((2, block, width, gathered * width), lambda k: (0, k, 0, 0)),
        compiler_params=pltpu.CompilerParams(vmem_limit_bytes=48 << 20),
        name="cross_spectra",
    )(rank_owned, power_all)


def body(rank_series, power_series, seg_offsets, bin_index):
    length = rank_series.shape[1]
    coarse = jnp.arange(0, length, FINE, dtype=jnp.int32)
    samples = jnp.concatenate([coarse, jnp.arange(FINE, dtype=jnp.int32)])
    grid = waves_of(bin_index, samples, length)
    back = waves_of(bin_index, -seg_offsets, length).reshape(4, -1, bin_index.shape[0])
    offset_rows = jnp.broadcast_to(seg_offsets.astype(jnp.float32)[None, :, None], (1,) + back.shape[1:])
    back = jnp.concatenate([back, offset_rows])
    power_all, rank_owned = exchange(grid, back, rank_series, power_series)
    return cross(rank_owned, power_all)


def solution(mesh):
    return jax.shard_map(
        body,
        mesh=mesh,
        in_specs=(
            P(("groups", "ch", "sub"), "seg"),
            P(("groups", "ch", "sub"), "seg"),
            P(("groups", "seg")),
            P(),
        ),
        out_specs=P(None, ("groups", "seg"), ("ch", "sub"), None),
        check_vma=False,
    )
```
